256 devices in a mesh: row: 16 (over x, y), col: 16 (over z, core).
Axes of the slice: x: 4, y: 4, z: 8, core: 2. Of those that a mesh axis runs over, the one named last changes fastest.
Arguments:
- density: bfloat16 [24576, 24576], P('col', 'row')
- margin: bfloat16 [24576, 24576], P('row', 'col')
- density_mask: int32 [192, 192], P('col', 'row'), may hold values from 0 to 1, as said below
- margin_mask: int32 [192, 192], P('row', 'col'), may hold values from 0 to 1, as said below
- keep_mask: int32 [3, 192], replicated, may hold values 0 or 1
Outputs:
- purified: bfloat16 [384, 24576], P('col', 'row')
The draws below stay inside these ranges and needn't reach their ends.
Inputs may be any that keep to these rules, and one draw needn't show every extreme that they name: `density_mask`: block (i, j) is 1 where |i - j| <= 1 and 0 where |i - j| >= 96. `margin_mask`: block (i, j) is 1 where |i - j| <= 1 and 0 where |i - j| >= 96.
All inputs are finite; a program needn't handle non-finite values.
Results may differ from the reference program's by a relative error of at most 0.008.
Values may be sent and summed in bfloat16 or wider, within the bound.
No kernel may reach another device: no remote copies, remote signals or barrier semaphores. Data moves between devices by JAX's collectives and lax.ppermute only.
A program may use at most 64 MiB of HBM per device.

```python
import math
import jax
import jax.numpy as jnp

BLK = 128
SLAB_BLK = 3
WIN_BLK = 192


def band_pattern(key):
    blocks = jnp.arange(WIN_BLK, dtype=jnp.int32)
    distance = jnp.abs(blocks[:, None] - blocks[None, :])
    threshold = jnp.where(distance <= 1, 1000, jnp.maximum(0, 800 - 1600 * distance // WIN_BLK))
    raw_draw = jax.random.randint(key, (WIN_BLK, WIN_BLK), 0, 1000, dtype=jnp.int32)
    return (raw_draw < threshold).astype(jnp.int32)


def entries(key, spread):
    matrix_order = WIN_BLK * BLK
    values = jax.random.truncated_normal(key, -5.0, 5.0, (matrix_order, matrix_order), jnp.float32)
    return (values * spread).astype(jnp.bfloat16)


def draw_density(key, part):
    return entries(jax.random.fold_in(key, 303), 2.0 / math.sqrt(0.3 * WIN_BLK * BLK))


def draw_margin(key, part):
    return entries(jax.random.fold_in(key, 404), 1.0 / math.sqrt(0.3 * WIN_BLK * BLK))


def draw_density_mask(key, part):
    return band_pattern(jax.random.fold_in(key, 101))


def draw_margin_mask(key, part):
    return band_pattern(jax.random.fold_in(key, 202))


def place_ends(values, rng, least, high):
    place = [jax.random.randint(jax.random.fold_in(rng, axis), (), 0, length) for axis, length in enumerate(values.shape)]
    longest = values.shape.index(max(values.shape))
    neighbour = place[:longest] + [(place[longest] + 1) % values.shape[longest]] + place[longest + 1:]
    return values.at[tuple(place)].set(least).at[tuple(neighbour)].set(high)


def setup_inputs(seed: int = 0) -> dict:
    key_list = jax.random.split(jax.random.key(seed), 6)
    density = draw_density(jax.random.fold_in(key_list[5], 71), 0)
    margin = draw_margin(jax.random.fold_in(key_list[5], 71), 0)
    density_mask = draw_density_mask(jax.random.fold_in(key_list[5], 71), 0)
    margin_mask = draw_margin_mask(jax.random.fold_in(key_list[5], 71), 0)
    keep_mask = place_ends((jax.random.randint(key_list[4], (SLAB_BLK, WIN_BLK), 0, 5) < 4).astype(jnp.int32), jax.random.fold_in(key_list[4], 1), 0, 1)
    return dict(density=density, margin=margin, density_mask=density_mask, margin_mask=margin_mask, keep_mask=keep_mask)


def block_zero(values, pattern, row_blocks, col_blocks):
    blocked = values.reshape(row_blocks, BLK, col_blocks, BLK)
    blocked = jnp.where(pattern[:, None, :, None] > 0, blocked, jnp.zeros_like(blocked))
    return blocked.reshape(row_blocks * BLK, col_blocks * BLK)


def reference(density, margin, density_mask, margin_mask, keep_mask):
    matrix_order = WIN_BLK * BLK
    density_eff = block_zero(density, density_mask, WIN_BLK, WIN_BLK)
    margin_eff = block_zero(margin, margin_mask, WIN_BLK, WIN_BLK)
    diag_index = jnp.arange(matrix_order).astype(jnp.int32)
    diagonal = (margin_eff[diag_index, diag_index].astype(jnp.float32) + 1.0).astype(jnp.bfloat16)
    margin_eff = margin_eff.at[diag_index, diag_index].set(diagonal)
    slab_left = density_eff[: SLAB_BLK * BLK, :]
    product_one = jnp.dot(slab_left, margin_eff, preferred_element_type=jnp.float32).astype(jnp.bfloat16)
    product_two = jnp.dot(product_one, density_eff, preferred_element_type=jnp.float32).astype(jnp.bfloat16)
    product_three = jnp.dot(product_two, margin_eff, preferred_element_type=jnp.float32).astype(jnp.bfloat16)
    product_four = jnp.dot(product_three, density_eff, preferred_element_type=jnp.float32)
    combined = 3.0 * product_two.astype(jnp.float32) - 2.0 * product_four
    combined = combined.reshape(SLAB_BLK, BLK, WIN_BLK, BLK)
    combined = jnp.where(keep_mask[:, None, :, None] > 0, combined, jnp.zeros_like(combined))
    return combined.reshape(SLAB_BLK * BLK, matrix_order).astype(jnp.bfloat16)
```

```python
import jax
import jax.numpy as jnp
from jax import lax
from jax.experimental import pallas as pl
from jax.experimental.pallas import tpu as pltpu
from jax.sharding import Mesh, PartitionSpec as P

BLK = 128
SLAB_BLK = 3
NX, NY, NZ, NC = 4, 4, 8, 2
ROW = ("x", "y")
BF = jnp.bfloat16
F32 = jnp.float32


def mask_kernel(with_diag, pattern_ref, where_ref, tile_ref, out_ref):
    i = pl.program_id(0)
    for j in range(tile_ref.shape[1] // BLK):
        cols = slice(j * BLK, (j + 1) * BLK)
        block = tile_ref[:, cols]
        block = jnp.where(pattern_ref[i, j] > 0, block, jnp.zeros_like(block))
        if with_diag:
            same = (where_ref[0] + i == where_ref[1] + j).astype(F32)
            eye = (
                lax.broadcasted_iota(jnp.int32, (BLK, BLK), 0)
                == lax.broadcasted_iota(jnp.int32, (BLK, BLK), 1)
            ).astype(F32)
            block = (block.astype(F32) + eye * same).astype(BF)
        out_ref[:, cols] = block


def masked(tile, pattern, place, rows, with_diag):
    cols = tile.shape[1]
    return pl.pallas_call(
        lambda *refs: mask_kernel(with_diag, *refs),
        grid=(rows // BLK,),
        in_specs=[
            pl.BlockSpec(memory_space=pltpu.SMEM),
            pl.BlockSpec(memory_space=pltpu.SMEM),
            pl.BlockSpec((BLK, cols), lambda i: (i, 0)),
        ],
        out_specs=pl.BlockSpec((BLK, cols), lambda i: (i, 0)),
        out_shape=jax.ShapeDtypeStruct((rows, cols), BF),
        cost_estimate=pl.CostEstimate(
            flops=rows * cols, bytes_accessed=4 * rows * cols, transcendentals=0
        ),
        name="mask_diag" if with_diag else "mask",
    )(pattern, place, tile)


def dot(a, b):
    return jnp.dot(a, b, preferred_element_type=F32)


def exchange(parts, axis):
    return lax.all_to_all(parts, axis, 0, 0, tiled=False)


def reduce_parts(parts, axis):
    return jnp.sum(exchange(parts, axis).astype(F32), axis=0)


def gather_parts(piece, axis, n):
    return exchange(jnp.broadcast_to(piece[None], (n,) + piece.shape), axis)


def swap(x):
    return lax.ppermute(x, "core", [(0, 1), (1, 0)])


def body(density, margin, density_mask, margin_mask, keep_mask):
    side = density.shape[0]
    nr = NX * NY
    slab = SLAB_BLK * BLK
    piece = slab // (NZ * NC)
    half = NZ * piece
    r = lax.axis_index(ROW)
    z = lax.axis_index("z")
    core = lax.axis_index("core")
    c = z * NC + core
    blocks = side // BLK
    place = jnp.stack([r * blocks, c * blocks]).astype(jnp.int32)

    top = masked(density, density_mask, place, slab, False)
    top = top.reshape(NZ, NC, piece, side)
    sent = lax.ppermute(top[:, 1], "core", [(0, 1)])
    mine = jnp.where(core == 0, top[:, 0], sent)
    got = jnp.where(z == 0, mine[0], jnp.zeros_like(mine[0]))
    for d in range(1, NZ):
        got = got + lax.ppermute(mine[d], "z", [(0, d)])
    own = gather_parts(got, "z", NZ).reshape(half, side)
    left = jnp.concatenate([own, swap(own)], axis=0)

    dense = masked(density, density_mask, place, side, False)
    over = masked(margin, margin_mask, place, side, True)

    def times_margin(left_full):
        part = dot(left_full, over).astype(BF).reshape(nr, slab // nr, side)
        total = reduce_parts(part, ROW).astype(BF)
        return gather_parts(total, ROW, nr).reshape(slab, side)

    def times_density(left_full):
        part = dot(left_full, dense)
        other = swap(part[half:].astype(BF))
        part = (part[:half] + other.astype(F32)).astype(BF)
        return reduce_parts(part.reshape(NZ, piece, side), "z")

    one = times_margin(left)
    two = times_density(one).astype(BF)
    own = gather_parts(two, "z", NZ).reshape(half, side)
    three = times_margin(jnp.concatenate([own, swap(own)], axis=0))
    four = times_density(three)

    rows = c * piece + lax.broadcasted_iota(jnp.int32, (piece, SLAB_BLK), 0)
    pick = (rows // BLK == lax.broadcasted_iota(jnp.int32, (piece, SLAB_BLK), 1)).astype(F32)
    keep = lax.dynamic_slice_in_dim(keep_mask, r * blocks, blocks, 1).astype(F32)
    spread = (
        lax.broadcasted_iota(jnp.int32, (blocks, side), 1) // BLK
        == lax.broadcasted_iota(jnp.int32, (blocks, side), 0)
    ).astype(F32)
    keep = dot(dot(pick, keep), spread)
    combined = 3.0 * two.astype(F32) - 2.0 * four
    return jnp.where(keep > 0.5, combined, 0.0).astype(BF)


def solution(mesh):
    grid = Mesh(mesh.devices.reshape(NX, NY, NZ, NC), ("x", "y", "z", "core"))
    dn, mg = P(("z", "core"), ROW), P(ROW, ("z", "core"))
    return jax.shard_map(
        body, mesh=grid, in_specs=(dn, mg, dn, mg, P()), out_specs=dn, check_vma=False
    )
```

```python
import jax
import jax.numpy as jnp
from jax import lax
from jax.experimental import pallas as pl
from jax.experimental.pallas import tpu as pltpu
from jax.sharding import Mesh, PartitionSpec as P

BLK = 128
SLAB_BLK = 3
NX, NY, NZ, NC = 4, 4, 8, 2
ROW = ("x", "y")
BF = jnp.bfloat16
F32 = jnp.float32
SMALL = 8 * 1024 * 1024


def mask_kernel(with_diag, pattern_ref, where_ref, tile_ref, out_ref):
    rows, cols = tile_ref.shape
    first = pl.program_id(0) * (rows // BLK)
    for i in range(rows // BLK):
        for j in range(cols // BLK):
            here = (slice(i * BLK, (i + 1) * BLK), slice(j * BLK, (j + 1) * BLK))
            stored = pattern_ref[first + i, j] > 0

            @pl.when(stored)
            def _():
                out_ref[here] = tile_ref[here]

            @pl.when(jnp.logical_not(stored))
            def _():
                out_ref[here] = jnp.zeros((BLK, BLK), BF)

            if with_diag:

                @pl.when(where_ref[0] + first + i == where_ref[1] + j)
                def _():
                    eye = (
                        lax.broadcasted_iota(jnp.int32, (BLK, BLK), 0)
                        == lax.broadcasted_iota(jnp.int32, (BLK, BLK), 1)
                    ).astype(F32)
                    out_ref[here] = (out_ref[here].astype(F32) + eye).astype(BF)


def masked(tile, pattern, place, with_diag):
    rows, cols = tile.shape
    step = 2 * BLK
    return pl.pallas_call(
        lambda *refs: mask_kernel(with_diag, *refs),
        grid=(rows // step,),
        in_specs=[
            pl.BlockSpec(memory_space=pltpu.SMEM),
            pl.BlockSpec(memory_space=pltpu.SMEM),
            pl.BlockSpec((step, cols), lambda i: (i, 0)),
        ],
        out_specs=pl.BlockSpec((step, cols), lambda i: (i, 0)),
        out_shape=jax.ShapeDtypeStruct((rows, cols), BF),
        cost_estimate=pl.CostEstimate(
            flops=rows * cols, bytes_accessed=4 * rows * cols, transcendentals=0
        ),
        name="mask_diag" if with_diag else "mask",
    )(pattern, place, pltpu.with_memory_space_constraint(tile, pltpu.HBM))


def slab_kernel(piece, pattern_ref, tile_ref, first_ref, second_ref, held, sems):
    rows, cols = held.shape
    parts = rows // BLK
    copies = []
    for p in range(parts):
        span = pl.ds(p * BLK, BLK)
        copies.append(pltpu.make_async_copy(tile_ref.at[span], held.at[span], sems.at[p]))
        copies[-1].start()
    for p in range(parts):
        copies[p].wait()
        stored = [pattern_ref[p, j] > 0 for j in range(cols // BLK)]
        for row in range(p * BLK, (p + 1) * BLK, 8):
            whose, at = divmod(row, piece)
            z, core = divmod(whose, NC)
            out_ref = (first_ref, second_ref)[core]
            for j in range(cols // BLK):
                lanes = slice(j * BLK, (j + 1) * BLK)
                block = held[row : row + 8, lanes]
                out_ref[z, at : at + 8, lanes] = jnp.where(stored[j], block, jnp.zeros_like(block))


def slab_halves(tile, pattern, slab, piece):
    cols = tile.shape[1]
    return pl.pallas_call(
        lambda *refs: slab_kernel(piece, *refs),
        in_specs=[
            pl.BlockSpec(memory_space=pltpu.SMEM),
            pl.BlockSpec(memory_space=pltpu.HBM),
        ],
        out_specs=[pl.BlockSpec(memory_space=pltpu.VMEM)] * NC,
        out_shape=[pltpu.VMEM((NZ, piece, cols), BF)] * NC,
        scratch_shapes=[pltpu.VMEM((slab, cols), BF), pltpu.SemaphoreType.DMA((SLAB_BLK,))],
        compiler_params=pltpu.CompilerParams(vmem_limit_bytes=SMALL),
        name="slab",
    )(pattern, pltpu.with_memory_space_constraint(tile, pltpu.HBM))


def dot_kernel(own_ref, other_ref, right_ref, own_out, other_out, held, sems):
    wide = held.shape[2]
    rows = own_ref.shape[0]
    copies = []
    for j in range(held.shape[0]):
        cols = pl.ds(j * wide, wide)
        copies.append(pltpu.make_async_copy(right_ref.at[:, cols], held.at[j], sems.at[j]))
        copies[-1].start()
    left = jnp.concatenate([own_ref[...], other_ref[...]], axis=0)
    for j in range(held.shape[0]):
        copies[j].wait()
        cols = slice(j * wide, (j + 1) * wide)
        sums = jnp.dot(left, held[j], preferred_element_type=F32)
        if other_out is None:
            own_out[:, cols] = sums.astype(BF)
        else:
            own_out[:, cols] = sums[:rows]
            other_out[:, cols] = sums[rows:].astype(BF)


def dot(own, other, right, apart):
    rows, depth = own.shape
    cols = right.shape[1]
    wide = 4 * BLK
    if apart:
        kernel, outs = dot_kernel, [pltpu.VMEM((rows, cols), F32), pltpu.VMEM((rows, cols), BF)]
    else:
        kernel = lambda a, b, c, out, *scratch: dot_kernel(a, b, c, out, None, *scratch)
        outs = [pltpu.VMEM((2 * rows, cols), BF)]
    return pl.pallas_call(
        kernel,
        in_specs=[pl.BlockSpec(memory_space=pltpu.VMEM)] * 2 + [pl.BlockSpec(memory_space=pltpu.HBM)],
        out_specs=[pl.BlockSpec(memory_space=pltpu.VMEM)] * len(outs),
        out_shape=outs,
        scratch_shapes=[
            pltpu.VMEM((cols // wide, depth, wide), BF),
            pltpu.SemaphoreType.DMA((cols // wide,)),
        ],
        compiler_params=pltpu.CompilerParams(vmem_limit_bytes=2 * SMALL),
        cost_estimate=pl.CostEstimate(
            flops=4 * rows * cols * depth, bytes_accessed=2 * cols * depth, transcendentals=0
        ),
        name="dot",
    )(
        pltpu.with_memory_space_constraint(own, pltpu.VMEM),
        pltpu.with_memory_space_constraint(other, pltpu.VMEM),
        pltpu.with_memory_space_constraint(right, pltpu.HBM),
    )


def exchange(parts, axis):
    return lax.all_to_all(parts, axis, 0, 0, tiled=False)


def swap(x):
    return lax.ppermute(x, "core", [(0, 1), (1, 0)])


def body(density, margin, density_mask, margin_mask, keep_mask):
    side = density.shape[0]
    nr = NX * NY
    slab = SLAB_BLK * BLK
    piece = slab // (NZ * NC)
    half = NZ * piece
    r = lax.axis_index(ROW)
    z = lax.axis_index("z")
    core = lax.axis_index("core")
    c = z * NC + core
    blocks = side // BLK
    place = jnp.stack([r * blocks, c * blocks]).astype(jnp.int32)

    def everywhere(rows, axis, n):
        return exchange(jnp.broadcast_to(rows[None], (n,) + rows.shape), axis)

    def total(parts):
        return jnp.sum(parts.astype(F32), axis=0)

    top = slab_halves(density, density_mask, slab, piece)
    mine = jnp.where(core == 0, top[0], lax.ppermute(top[1], "core", [(0, 1)]))
    got = jnp.where(z == 0, mine[0], jnp.zeros_like(mine[0]))
    for d in range(1, NZ):
        got = got + lax.ppermute(mine[d], "z", [(0, d)])
    own = everywhere(got, "z", NZ).reshape(half, side)

    over = masked(margin, margin_mask, place, True)
    own, over = lax.optimization_barrier((own, over))
    dense = masked(density, density_mask, place, False)

    def times_margin(own):
        (part,) = dot(own, swap(own), over, False)
        rows = total(exchange(part.reshape(nr, slab // nr, side), ROW)).astype(BF)
        return everywhere(rows, ROW, nr).reshape(slab, side)

    def times_density(left):
        part, other = dot(left[:half], left[half:], dense, True)
        part = (part + swap(other).astype(F32)).astype(BF)
        return total(exchange(part.reshape(NZ, piece, side), "z"))

    two = times_density(times_margin(own)).astype(BF)
    own = everywhere(two, "z", NZ).reshape(half, side)
    four = times_density(times_margin(own))

    rows = c * piece + lax.broadcasted_iota(jnp.int32, (piece, SLAB_BLK), 0)
    pick = (rows // BLK == lax.broadcasted_iota(jnp.int32, (piece, SLAB_BLK), 1)).astype(F32)
    keep = lax.dynamic_slice_in_dim(keep_mask, r * blocks, blocks, 1).astype(F32)
    wide = (
        lax.broadcasted_iota(jnp.int32, (blocks, side), 1) // BLK
        == lax.broadcasted_iota(jnp.int32, (blocks, side), 0)
    ).astype(F32)
    keep = jnp.dot(jnp.dot(pick, keep), wide)
    combined = 3.0 * two.astype(F32) - 2.0 * four
    return jnp.where(keep > 0.5, combined, 0.0).astype(BF)


def solution(mesh):
    grid = Mesh(mesh.devices.reshape(NX, NY, NZ, NC), ("x", "y", "z", "core"))
    dn, mg = P(("z", "core"), ROW), P(ROW, ("z", "core"))
    return jax.shard_map(
        body, mesh=grid, in_specs=(dn, mg, dn, mg, P()), out_specs=dn, check_vma=False
    )
```

```python
import jax
import jax.numpy as jnp
from jax import lax
from jax.experimental import pallas as pl
from jax.experimental.pallas import tpu as pltpu
from jax.sharding import Mesh, PartitionSpec as P

BLK = 128
SLAB_BLK = 3
NX, NY, NZ, NC = 4, 4, 8, 2
ROW = ("x", "y")
BF = jnp.bfloat16
F32 = jnp.float32
SMALL = 8 * 1024 * 1024


def slab_kernel(piece, pattern_ref, tile_ref, first_ref, second_ref, held, sems):
    rows, cols = held.shape
    parts = rows // BLK
    copies = []
    for p in range(parts):
        span = pl.ds(p * BLK, BLK)
        copies.append(pltpu.make_async_copy(tile_ref.at[span], held.at[span], sems.at[p]))
        copies[-1].start()
    for p in range(parts):
        copies[p].wait()
        stored = [pattern_ref[p, j] > 0 for j in range(cols // BLK)]
        for row in range(p * BLK, (p + 1) * BLK, 8):
            whose, at = divmod(row, piece)
            z, core = divmod(whose, NC)
            out_ref = (first_ref, second_ref)[core]
            for j in range(cols // BLK):
                lanes = slice(j * BLK, (j + 1) * BLK)
                block = held[row : row + 8, lanes]
                out_ref[z, at : at + 8, lanes] = jnp.where(stored[j], block, jnp.zeros_like(block))


def slab_halves(tile, pattern, slab, piece):
    cols = tile.shape[1]
    return pl.pallas_call(
        lambda *refs: slab_kernel(piece, *refs),
        in_specs=[
            pl.BlockSpec(memory_space=pltpu.SMEM),
            pl.BlockSpec(memory_space=pltpu.HBM),
        ],
        out_specs=[pl.BlockSpec(memory_space=pltpu.VMEM)] * NC,
        out_shape=[pltpu.VMEM((NZ, piece, cols), BF)] * NC,
        scratch_shapes=[pltpu.VMEM((slab, cols), BF), pltpu.SemaphoreType.DMA((SLAB_BLK,))],
        compiler_params=pltpu.CompilerParams(vmem_limit_bytes=SMALL),
        name="slab",
    )(pattern, pltpu.with_memory_space_constraint(tile, pltpu.HBM))


def load_kernel(with_diag, pattern_ref, where_ref, left_ref, right_ref, out_ref, held, sems):
    depth, width = held.shape
    parts = sems.shape[0]
    wide = width // parts
    copies = [
        pltpu.make_async_copy(
            right_ref.at[:, pl.ds(j * wide, wide)], held.at[:, pl.ds(j * wide, wide)], sems.at[j]
        )
        for j in range(parts)
    ]
    copies[0].start()
    copies[1].start()
    for p in range(parts):
        copies[p].wait()
        if p + 2 < parts:
            copies[p + 2].start()
        for j in range(p * wide // BLK, (p + 1) * wide // BLK):
            for i in range(depth // BLK):
                here = (slice(i * BLK, (i + 1) * BLK), slice(j * BLK, (j + 1) * BLK))

                @pl.when(pattern_ref[i, j] <= 0)
                def _():
                    held[here] = jnp.zeros((BLK, BLK), BF)

                if with_diag and i == j:

                    @pl.when(where_ref[0] == where_ref[1])
                    def _():
                        eye = (
                            lax.broadcasted_iota(jnp.int32, (BLK, BLK), 0)
                            == lax.broadcasted_iota(jnp.int32, (BLK, BLK), 1)
                        ).astype(F32)
                        held[here] = (held[here].astype(F32) + eye).astype(BF)

        cols = slice(p * wide, (p + 1) * wide)
        out_ref[:, cols] = jnp.dot(
            left_ref[...], held[:, cols], preferred_element_type=F32
        ).astype(BF)


def in_vmem(x):
    return pltpu.with_memory_space_constraint(x, pltpu.VMEM)


def in_hbm(x):
    return pltpu.with_memory_space_constraint(x, pltpu.HBM)


VMEM_SPEC = pl.BlockSpec(memory_space=pltpu.VMEM)
SMEM_SPEC = pl.BlockSpec(memory_space=pltpu.SMEM)
HBM_SPEC = pl.BlockSpec(memory_space=pltpu.HBM)


def load_dot(left, right, pattern, place, with_diag):
    rows = left.shape[0]
    depth, cols = right.shape
    return pl.pallas_call(
        lambda *refs: load_kernel(with_diag, *refs),
        in_specs=[SMEM_SPEC, SMEM_SPEC, VMEM_SPEC, HBM_SPEC],
        out_specs=[VMEM_SPEC, VMEM_SPEC],
        out_shape=[pltpu.VMEM((rows, cols), BF), pltpu.VMEM((depth, cols), BF)],
        scratch_shapes=[pltpu.SemaphoreType.DMA((3,))],
        compiler_params=pltpu.CompilerParams(vmem_limit_bytes=SMALL),
        cost_estimate=pl.CostEstimate(
            flops=2 * rows * cols * depth, bytes_accessed=2 * cols * depth, transcendentals=0
        ),
        name="load_dot",
    )(pattern, place, in_vmem(left), in_hbm(right))


def dot_kernel(left_ref, right_ref, out_ref):
    wide = 4 * BLK
    for p in range(right_ref.shape[1] // wide):
        cols = slice(p * wide, (p + 1) * wide)
        out_ref[:, cols] = jnp.dot(
            left_ref[...], right_ref[:, cols], preferred_element_type=F32
        ).astype(out_ref.dtype)


def dot(left, right, dtype):
    rows, depth = left.shape
    cols = right.shape[1]
    return pl.pallas_call(
        dot_kernel,
        in_specs=[VMEM_SPEC, VMEM_SPEC],
        out_specs=VMEM_SPEC,
        out_shape=pltpu.VMEM((rows, cols), dtype),
        compiler_params=pltpu.CompilerParams(vmem_limit_bytes=SMALL),
        cost_estimate=pl.CostEstimate(
            flops=2 * rows * cols * depth, bytes_accessed=2 * rows * (cols + depth), transcendentals=0
        ),
        name="dot",
    )(in_vmem(left), right)


def sum_kernel(parts_ref, out_ref):
    n, rows, cols = parts_ref.shape
    for j in range(cols // BLK):
        lanes = slice(j * BLK, (j + 1) * BLK)
        total = parts_ref[0, :, lanes].astype(F32)
        for k in range(1, n):
            total = total + parts_ref[k, :, lanes].astype(F32)
        for k in range(n):
            out_ref[k, :, lanes] = total.astype(BF)


def summed(parts):
    return pl.pallas_call(
        sum_kernel,
        in_specs=[VMEM_SPEC],
        out_specs=VMEM_SPEC,
        out_shape=pltpu.VMEM(parts.shape, BF),
        compiler_params=pltpu.CompilerParams(vmem_limit_bytes=SMALL),
        name="sum",
    )(in_vmem(parts))


def finish_kernel(keep_ref, where_ref, parts_ref, two_ref, out_ref):
    n, rows, cols = parts_ref.shape
    for at in range(0, rows, 8):
        block_row = (where_ref[2] + at) // BLK
        for j in range(cols // BLK):
            lanes = slice(j * BLK, (j + 1) * BLK)
            four = parts_ref[0, at : at + 8, lanes].astype(F32)
            for k in range(1, n):
                four = four + parts_ref[k, at : at + 8, lanes].astype(F32)
            value = 3.0 * two_ref[at : at + 8, lanes].astype(F32) - 2.0 * four
            kept = keep_ref[block_row, where_ref[3] + j] > 0
            out_ref[at : at + 8, lanes] = jnp.where(kept, value, jnp.zeros_like(value)).astype(BF)


def finish(parts, two, keep, place):
    return pl.pallas_call(
        finish_kernel,
        in_specs=[SMEM_SPEC, SMEM_SPEC, VMEM_SPEC, VMEM_SPEC],
        out_specs=VMEM_SPEC,
        out_shape=jax.ShapeDtypeStruct(two.shape, BF),
        compiler_params=pltpu.CompilerParams(vmem_limit_bytes=SMALL),
        name="finish",
    )(keep, place, in_vmem(parts), in_vmem(two))


def exchange(parts, axis):
    return lax.all_to_all(parts, axis, 0, 0, tiled=False)


def swap(x):
    return lax.ppermute(x, "core", [(0, 1), (1, 0)])


def body(density, margin, density_mask, margin_mask, keep_mask):
    side = density.shape[0]
    nr = NX * NY
    r = lax.axis_index(ROW)
    z = lax.axis_index("z")
    core = lax.axis_index("core")
    c = z * NC + core
    blocks = side // BLK
    slab = SLAB_BLK * BLK
    piece = slab // (NZ * NC)
    place = jnp.stack([r * blocks, c * blocks, c * piece, r * blocks]).astype(jnp.int32)

    half = NZ * piece

    top = slab_halves(density, density_mask, slab, piece)
    mine = jnp.where(core == 0, top[0], lax.ppermute(top[1], "core", [(0, 1)]))
    got = jnp.where(z == 0, mine[0], jnp.zeros_like(mine[0]))
    for d in sorted(range(1, NZ), key=lambda d: min(d, NZ - d)):
        got = got + lax.ppermute(mine[d], "z", [(0, d)])
    own = exchange(jnp.broadcast_to(got[None], (NZ, piece, side)), "z").reshape(half, side)

    def over_rows(first, second):
        part = jnp.concatenate([first, second]).reshape(nr, slab // nr, side)
        return exchange(summed(exchange(part, ROW)), ROW).reshape(slab, side)

    def over_cols(kept, sent):
        part = (kept + sent.astype(F32)).astype(BF)
        return exchange(part.reshape(NZ, piece, side), "z")

    other = swap(own)
    first, over = load_dot(own, margin, margin_mask, place, True)
    left = over_rows(first, dot(other, over, BF))
    sent, dense = load_dot(left[half:], density, density_mask, place, False)
    sent = swap(sent)
    twos = summed(over_cols(dot(left[:half], dense, F32), sent))
    two = twos[0]
    own = exchange(twos, "z").reshape(half, side)
    other = swap(own)
    first = dot(own, over, BF)
    left = over_rows(first, dot(other, over, BF))
    sent = swap(dot(left[half:], dense, BF))
    parts = over_cols(dot(left[:half], dense, F32), sent)
    return finish(parts, two, keep_mask, place)


def solution(mesh):
    grid = Mesh(mesh.devices.reshape(NX, NY, NZ, NC), ("x", "y", "z", "core"))
    dn, mg = P(("z", "core"), ROW), P(ROW, ("z", "core"))
    return jax.shard_map(
        body, mesh=grid, in_specs=(dn, mg, dn, mg, P()), out_specs=dn, check_vma=False
    )
```

```python
import jax
import jax.numpy as jnp
from jax import lax
from jax.experimental import pallas as pl
from jax.experimental.pallas import tpu as pltpu
from jax.sharding import Mesh, PartitionSpec as P


BLK = 128
SLAB_BLK = 3
NX, NY, NZ, NC = 4, 4, 8, 2
ROW = ("x", "y")
BF = jnp.bfloat16
F32 = jnp.float32
SMALL = 8 * 1024 * 1024
ORDER = (1, 2, 3, 6, 5, 7, 4)


def slab_kernel(piece, pattern_ref, tile_ref, first_ref, second_ref, held, sems):
    @pl.when(lax.axis_index("z") == 0)
    def _():
        rows, cols = held.shape
        parts = rows // BLK
        copies = []
        for p in range(parts):
            span = pl.ds(p * BLK, BLK)
            copies.append(pltpu.make_async_copy(tile_ref.at[span], held.at[span], sems.at[p]))
            copies[-1].start()
        for p in range(parts):
            copies[p].wait()
            stored = [pattern_ref[p, j] > 0 for j in range(cols // BLK)]
            for row in range(p * BLK, (p + 1) * BLK, 8):
                whose, at = divmod(row, piece)
                z, core = divmod(whose, NC)
                out_ref = (first_ref, second_ref)[core]
                for j in range(cols // BLK):
                    lanes = slice(j * BLK, (j + 1) * BLK)
                    block = held[row : row + 8, lanes]
                    out_ref[z, at : at + 8, lanes] = jnp.where(stored[j], block, jnp.zeros_like(block))


def slab_halves(tile, pattern, slab, piece):
    cols = tile.shape[1]
    return pl.pallas_call(
        lambda *refs: slab_kernel(piece, *refs),
        in_specs=[
            pl.BlockSpec(memory_space=pltpu.SMEM),
            pl.BlockSpec(memory_space=pltpu.HBM),
        ],
        out_specs=[pl.BlockSpec(memory_space=pltpu.VMEM)] * NC,
        out_shape=[pltpu.VMEM((NZ, piece, cols), BF)] * NC,
        scratch_shapes=[pltpu.VMEM((slab, cols), BF), pltpu.SemaphoreType.DMA((SLAB_BLK,))],
        compiler_params=pltpu.CompilerParams(vmem_limit_bytes=SMALL),
        name="slab",
    )(pattern, pltpu.with_memory_space_constraint(tile, pltpu.HBM))


def load_kernel(with_diag, pattern_ref, where_ref, left_ref, right_ref, out_ref, held, sems):
    depth, width = held.shape
    parts = sems.shape[0]
    wide = width // parts
    copies = [
        pltpu.make_async_copy(
            right_ref.at[:, pl.ds(j * wide, wide)], held.at[:, pl.ds(j * wide, wide)], sems.at[j]
        )
        for j in range(parts)
    ]
    copies[0].start()
    copies[1].start()
    for p in range(parts):
        copies[p].wait()
        if p + 2 < parts:
            copies[p + 2].start()
        for j in range(p * wide // BLK, (p + 1) * wide // BLK):
            for i in range(depth // BLK):
                here = (slice(i * BLK, (i + 1) * BLK), slice(j * BLK, (j + 1) * BLK))

                @pl.when(pattern_ref[i, j] <= 0)
                def _():
                    held[here] = jnp.zeros((BLK, BLK), BF)

                if with_diag and i == j:

                    @pl.when(where_ref[0] == where_ref[1])
                    def _():
                        eye = (
                            lax.broadcasted_iota(jnp.int32, (BLK, BLK), 0)
                            == lax.broadcasted_iota(jnp.int32, (BLK, BLK), 1)
                        ).astype(F32)
                        held[here] = (held[here].astype(F32) + eye).astype(BF)

        cols = slice(p * wide, (p + 1) * wide)
        out_ref[:, cols] = jnp.dot(
            left_ref[...], held[:, cols], preferred_element_type=F32
        ).astype(BF)


def in_vmem(x):
    return pltpu.with_memory_space_constraint(x, pltpu.VMEM)


def in_hbm(x):
    return pltpu.with_memory_space_constraint(x, pltpu.HBM)


VMEM_SPEC = pl.BlockSpec(memory_space=pltpu.VMEM)
SMEM_SPEC = pl.BlockSpec(memory_space=pltpu.SMEM)
HBM_SPEC = pl.BlockSpec(memory_space=pltpu.HBM)


def load_dot(left, right, pattern, place, with_diag):
    rows = left.shape[0]
    depth, cols = right.shape
    return pl.pallas_call(
        lambda *refs: load_kernel(with_diag, *refs),
        in_specs=[SMEM_SPEC, SMEM_SPEC, VMEM_SPEC, HBM_SPEC],
        out_specs=[VMEM_SPEC, VMEM_SPEC],
        out_shape=[pltpu.VMEM((rows, cols), BF), pltpu.VMEM((depth, cols), BF)],
        scratch_shapes=[pltpu.SemaphoreType.DMA((3,))],
        compiler_params=pltpu.CompilerParams(vmem_limit_bytes=SMALL),
        cost_estimate=pl.CostEstimate(
            flops=2 * rows * cols * depth, bytes_accessed=2 * cols * depth, transcendentals=0
        ),
        name="load_dot",
    )(pattern, place, in_vmem(left), in_hbm(right))


def dot_kernel(left_ref, right_ref, out_ref):
    wide = 4 * BLK
    for p in range(right_ref.shape[1] // wide):
        cols = slice(p * wide, (p + 1) * wide)
        out_ref[:, cols] = jnp.dot(
            left_ref[...], right_ref[:, cols], preferred_element_type=F32
        ).astype(out_ref.dtype)


def dot(left, right, dtype):
    rows, depth = left.shape
    cols = right.shape[1]
    return pl.pallas_call(
        dot_kernel,
        in_specs=[VMEM_SPEC, VMEM_SPEC],
        out_specs=VMEM_SPEC,
        out_shape=pltpu.VMEM((rows, cols), dtype),
        compiler_params=pltpu.CompilerParams(vmem_limit_bytes=SMALL),
        cost_estimate=pl.CostEstimate(
            flops=2 * rows * cols * depth, bytes_accessed=2 * rows * (cols + depth), transcendentals=0
        ),
        name="dot",
    )(in_vmem(left), right)


def sum_kernel(parts_ref, out_ref):
    n, _, cols = parts_ref.shape
    for j in range(cols // BLK):
        lanes = slice(j * BLK, (j + 1) * BLK)
        total = parts_ref[0, :, lanes].astype(F32)
        for k in range(1, n):
            total = total + parts_ref[k, :, lanes].astype(F32)
        for k in range(n):
            out_ref[k, :, lanes] = total.astype(BF)


def summed(parts):
    return pl.pallas_call(
        sum_kernel,
        in_specs=[VMEM_SPEC],
        out_specs=VMEM_SPEC,
        out_shape=pltpu.VMEM(parts.shape, BF),
        compiler_params=pltpu.CompilerParams(vmem_limit_bytes=SMALL),
        name="sum",
    )(in_vmem(parts))


def finish_kernel(keep_ref, where_ref, parts_ref, two_ref, out_ref):
    n, rows, cols = parts_ref.shape
    for at in range(0, rows, 8):
        block_row = (where_ref[2] + at) // BLK
        for j in range(cols // BLK):
            lanes = slice(j * BLK, (j + 1) * BLK)
            four = parts_ref[0, at : at + 8, lanes].astype(F32)
            for k in range(1, n):
                four = four + parts_ref[k, at : at + 8, lanes].astype(F32)
            value = 3.0 * two_ref[0, at : at + 8, lanes].astype(F32) - 2.0 * four
            kept = keep_ref[block_row, where_ref[3] + j] > 0
            out_ref[at : at + 8, lanes] = jnp.where(kept, value, jnp.zeros_like(value)).astype(BF)


def finish(parts, two, keep, place):
    return pl.pallas_call(
        finish_kernel,
        in_specs=[SMEM_SPEC, SMEM_SPEC, VMEM_SPEC, VMEM_SPEC],
        out_specs=VMEM_SPEC,
        out_shape=jax.ShapeDtypeStruct(two.shape[1:], BF),
        compiler_params=pltpu.CompilerParams(vmem_limit_bytes=SMALL),
        name="finish",
    )(keep, place, in_vmem(parts), in_vmem(two))


def exchange(parts, axis):
    return lax.all_to_all(parts, axis, 0, 0, tiled=False)


def swap(x):
    return lax.ppermute(x, "core", [(0, 1), (1, 0)])


def body(density, margin, density_mask, margin_mask, keep_mask):
    side = density.shape[0]
    nr = NX * NY
    r = lax.axis_index(ROW)
    z = lax.axis_index("z")
    core = lax.axis_index("core")
    c = z * NC + core
    blocks = side // BLK
    slab = SLAB_BLK * BLK
    piece = slab // (NZ * NC)
    place = jnp.stack([r * blocks, c * blocks, c * piece, r * blocks]).astype(jnp.int32)

    half = NZ * piece

    top = slab_halves(density, density_mask, slab, piece)
    mine = jnp.where(core == 0, top[0], lax.ppermute(top[1], ("z", "core"), [(0, 1)]))
    got = jnp.where(z == 0, mine[0], jnp.zeros_like(mine[0]))
    for d in ORDER:
        dealt = lax.ppermute(mine[d], "z", [(0, d)])
        got = got + dealt
    own = exchange(jnp.broadcast_to(got[None], (NZ, piece, side)), "z").reshape(half, side)

    def over_rows(first, second):
        part = jnp.concatenate([first, second]).reshape(nr, slab // nr, side)
        return exchange(summed(exchange(part, ROW)), ROW).reshape(slab, side)

    def over_cols(kept, sent):
        part = (kept + sent.astype(F32)).astype(BF)
        return exchange(part.reshape(NZ, piece, side), "z")

    other = swap(own)
    first, over = load_dot(own, margin, margin_mask, place, True)
    left = over_rows(first, dot(other, over, BF))
    sent, dense = load_dot(left[half:], density, density_mask, place, False)
    sent = swap(sent)
    twos = summed(over_cols(dot(left[:half], dense, F32), sent))
    own = exchange(twos, "z").reshape(half, side)
    other = swap(own)
    first = dot(own, over, BF)
    left = over_rows(first, dot(other, over, BF))
    sent = swap(dot(left[half:], dense, BF))
    parts = over_cols(dot(left[:half], dense, F32), sent)
    return finish(parts, twos, keep_mask, place)


def solution(mesh):
    grid = Mesh(mesh.devices.reshape(NX, NY, NZ, NC), ("x", "y", "z", "core"))
    dn, mg = P(("z", "core"), ROW), P(ROW, ("z", "core"))
    return jax.shard_map(
        body, mesh=grid, in_specs=(dn, mg, dn, mg, P()), out_specs=dn, check_vma=False
    )
```

```python
import jax
import jax.numpy as jnp
from jax import lax
from jax.experimental import pallas as pl
from jax.experimental.pallas import tpu as pltpu
from jax.sharding import Mesh, PartitionSpec as P


BLK = 128
SLAB_BLK = 3
NX, NY, NZ, NC = 4, 4, 8, 2
ROW = ("x", "y")
BF = jnp.bfloat16
F32 = jnp.float32
SMALL = 8 * 1024 * 1024
ORDER = (1, 2, 3, 6, 5, 7, 4)


def slab_kernel(piece, pattern_ref, tile_ref, first_ref, second_ref, held, sems):
    @pl.when(lax.axis_index("z") == 0)
    def _():
        rows, cols = held.shape
        parts = rows // BLK
        copies = []
        for p in range(parts):
            span = pl.ds(p * BLK, BLK)
            copies.append(pltpu.make_async_copy(tile_ref.at[span], held.at[span], sems.at[p]))
            copies[-1].start()
        for p in range(parts):
            copies[p].wait()
            stored = [pattern_ref[p, j] > 0 for j in range(cols // BLK)]
            for row in range(p * BLK, (p + 1) * BLK, 8):
                whose, at = divmod(row, piece)
                z, core = divmod(whose, NC)
                out_ref = (first_ref, second_ref)[core]
                for j in range(cols // BLK):
                    lanes = slice(j * BLK, (j + 1) * BLK)
                    block = held[row : row + 8, lanes]
                    out_ref[z, at : at + 8, lanes] = jnp.where(stored[j], block, jnp.zeros_like(block))


def slab_halves(tile, pattern, slab, piece):
    cols = tile.shape[1]
    return pl.pallas_call(
        lambda *refs: slab_kernel(piece, *refs),
        in_specs=[
            pl.BlockSpec(memory_space=pltpu.SMEM),
            pl.BlockSpec(memory_space=pltpu.HBM),
        ],
        out_specs=[pl.BlockSpec(memory_space=pltpu.VMEM)] * NC,
        out_shape=[pltpu.VMEM((NZ, piece, cols), BF)] * NC,
        scratch_shapes=[pltpu.VMEM((slab, cols), BF), pltpu.SemaphoreType.DMA((SLAB_BLK,))],
        compiler_params=pltpu.CompilerParams(vmem_limit_bytes=SMALL),
        name="slab",
    )(pltpu.with_memory_space_constraint(pattern, pltpu.HBM), pltpu.with_memory_space_constraint(tile, pltpu.HBM))


def grid_place():
    row = lax.axis_index("x") * NY + lax.axis_index("y")
    return row, lax.axis_index("z") * NC + lax.axis_index("core")


def load_kernel(with_diag, pattern_ref, left_ref, right_ref, out_ref, held, sems):
    depth, width = held.shape
    row, col = grid_place()
    diagonal = row == col
    parts = sems.shape[0]
    wide = width // parts
    tall = depth // sems.shape[1]
    copies = []
    for p in range(parts):
        for q in range(sems.shape[1]):
            span = (pl.ds(q * tall, tall), pl.ds(p * wide, wide))
            copies.append(
                pltpu.make_async_copy(right_ref.at[span], held.at[span], sems.at[p, q])
            )
            copies[-1].start()
    for p in range(parts):
        for q in range(sems.shape[1]):
            copies[p * sems.shape[1] + q].wait()
        blocks = range(p * wide // BLK, (p + 1) * wide // BLK)
        if with_diag:

            @pl.when(diagonal)
            def _():
                eye = (
                    lax.broadcasted_iota(jnp.int32, (BLK, BLK), 0)
                    == lax.broadcasted_iota(jnp.int32, (BLK, BLK), 1)
                ).astype(F32)
                for j in blocks:
                    here = (slice(j * BLK, (j + 1) * BLK), slice(j * BLK, (j + 1) * BLK))
                    block = jnp.where(pattern_ref[j, j] > 0, held[here].astype(F32), 0.0)
                    held[here] = (block + eye).astype(BF)

        strips = []
        for i in range(depth // BLK):
            strip = []
            for j in blocks:
                block = held[i * BLK : (i + 1) * BLK, j * BLK : (j + 1) * BLK]
                stored = pattern_ref[i, j] > 0
                if with_diag and i == j:
                    stored = jnp.logical_or(stored, diagonal)
                strip.append(jnp.where(stored, block, jnp.zeros_like(block)))
            strips.append(jnp.concatenate(strip, axis=1))
        values = jnp.concatenate(strips, axis=0)
        cols = slice(p * wide, (p + 1) * wide)
        held[:, cols] = values
        out_ref[:, cols] = jnp.dot(left_ref[...], values, preferred_element_type=F32).astype(BF)


def in_vmem(x):
    return pltpu.with_memory_space_constraint(x, pltpu.VMEM)


def in_hbm(x):
    return pltpu.with_memory_space_constraint(x, pltpu.HBM)


VMEM_SPEC = pl.BlockSpec(memory_space=pltpu.VMEM)
SMEM_SPEC = pl.BlockSpec(memory_space=pltpu.SMEM)
HBM_SPEC = pl.BlockSpec(memory_space=pltpu.HBM)


def load_dot(left, right, pattern, with_diag):
    rows = left.shape[0]
    depth, cols = right.shape
    return pl.pallas_call(
        lambda *refs: load_kernel(with_diag, *refs),
        in_specs=[SMEM_SPEC, VMEM_SPEC, HBM_SPEC],
        out_specs=[VMEM_SPEC, VMEM_SPEC],
        out_shape=[pltpu.VMEM((rows, cols), BF), pltpu.VMEM((depth, cols), BF)],
        scratch_shapes=[pltpu.SemaphoreType.DMA((3, 4))],
        compiler_params=pltpu.CompilerParams(vmem_limit_bytes=SMALL),
        cost_estimate=pl.CostEstimate(
            flops=2 * rows * cols * depth, bytes_accessed=2 * cols * depth, transcendentals=0
        ),
        name="load_dot",
    )(in_hbm(pattern), in_vmem(left), in_hbm(right))


def dot_kernel(left_ref, right_ref, out_ref):
    wide = 4 * BLK
    for p in range(right_ref.shape[1] // wide):
        cols = slice(p * wide, (p + 1) * wide)
        out_ref[:, cols] = jnp.dot(
            left_ref[...], right_ref[:, cols], preferred_element_type=F32
        ).astype(out_ref.dtype)


def dot(left, right, dtype):
    rows, depth = left.shape
    cols = right.shape[1]
    return pl.pallas_call(
        dot_kernel,
        in_specs=[VMEM_SPEC, VMEM_SPEC],
        out_specs=VMEM_SPEC,
        out_shape=pltpu.VMEM((rows, cols), dtype),
        compiler_params=pltpu.CompilerParams(vmem_limit_bytes=SMALL),
        cost_estimate=pl.CostEstimate(
            flops=2 * rows * cols * depth, bytes_accessed=2 * rows * (cols + depth), transcendentals=0
        ),
        name="dot",
    )(in_vmem(left), right)


def sum_kernel(parts_ref, out_ref):
    n, _, cols = parts_ref.shape
    for j in range(cols // BLK):
        lanes = slice(j * BLK, (j + 1) * BLK)
        total = parts_ref[0, :, lanes].astype(F32)
        for k in range(1, n):
            total = total + parts_ref[k, :, lanes].astype(F32)
        for k in range(n):
            out_ref[k, :, lanes] = total.astype(BF)


def summed(parts):
    return pl.pallas_call(
        sum_kernel,
        in_specs=[VMEM_SPEC],
        out_specs=VMEM_SPEC,
        out_shape=pltpu.VMEM(parts.shape, BF),
        compiler_params=pltpu.CompilerParams(vmem_limit_bytes=SMALL),
        name="sum",
    )(in_vmem(parts))


def finish_kernel(keep_ref, parts_ref, two_ref, out_ref):
    n, rows, cols = parts_ref.shape
    row, col = grid_place()
    for at in range(0, rows, 8):
        block_row = (col * rows + at) // BLK
        for j in range(cols // BLK):
            lanes = slice(j * BLK, (j + 1) * BLK)
            four = parts_ref[0, at : at + 8, lanes].astype(F32)
            for k in range(1, n):
                four = four + parts_ref[k, at : at + 8, lanes].astype(F32)
            value = 3.0 * two_ref[0, at : at + 8, lanes].astype(F32) - 2.0 * four
            kept = keep_ref[block_row, row * (cols // BLK) + j] > 0
            out_ref[at : at + 8, lanes] = jnp.where(kept, value, jnp.zeros_like(value)).astype(BF)


def finish(parts, two, keep):
    return pl.pallas_call(
        finish_kernel,
        in_specs=[SMEM_SPEC, VMEM_SPEC, VMEM_SPEC],
        out_specs=VMEM_SPEC,
        out_shape=jax.ShapeDtypeStruct(two.shape[1:], BF),
        compiler_params=pltpu.CompilerParams(vmem_limit_bytes=SMALL),
        name="finish",
    )(in_hbm(keep), in_vmem(parts), in_vmem(two))


def exchange(parts, axis):
    return lax.all_to_all(parts, axis, 0, 0, tiled=False)


def swap(x):
    return lax.ppermute(x, "core", [(0, 1), (1, 0)])


def body(density, margin, density_mask, margin_mask, keep_mask):
    side = density.shape[0]
    nr = NX * NY
    z = lax.axis_index("z")
    core = lax.axis_index("core")
    slab = SLAB_BLK * BLK
    piece = slab // (NZ * NC)
    half = NZ * piece

    top = slab_halves(density, density_mask, slab, piece)
    mine = jnp.where(core == 0, top[0], lax.ppermute(top[1], ("z", "core"), [(0, 1)]))
    got = jnp.where(z == 0, mine[0], jnp.zeros_like(mine[0]))
    for d in ORDER:
        dealt = lax.ppermute(mine[d], "z", [(0, d)])
        got = got + dealt
    own = exchange(jnp.broadcast_to(got[None], (NZ, piece, side)), "z").reshape(half, side)

    def over_rows(first, second):
        part = jnp.concatenate([first, second]).reshape(nr, slab // nr, side)
        return exchange(summed(exchange(part, ROW)), ROW).reshape(slab, side)

    def over_cols(kept, sent):
        part = (kept + sent.astype(F32)).astype(BF)
        return exchange(part.reshape(NZ, piece, side), "z")

    other = swap(own)
    first, over = load_dot(own, margin, margin_mask, True)
    left = over_rows(first, dot(other, over, BF))
    sent, dense = load_dot(left[half:], density, density_mask, False)
    sent = swap(sent)
    twos = summed(over_cols(dot(left[:half], dense, F32), sent))
    own = exchange(twos, "z").reshape(half, side)
    other = swap(own)
    first = dot(own, over, BF)
    left = over_rows(first, dot(other, over, BF))
    sent = swap(dot(left[half:], dense, BF))
    parts = over_cols(dot(left[:half], dense, F32), sent)
    return finish(parts, twos, keep_mask)


def solution(mesh):
    grid = Mesh(mesh.devices.reshape(NX, NY, NZ, NC), ("x", "y", "z", "core"))
    dn, mg = P(("z", "core"), ROW), P(ROW, ("z", "core"))
    return jax.shard_map(
        body, mesh=grid, in_specs=(dn, mg, dn, mg, P()), out_specs=dn, check_vma=False
    )
```

```python
import jax
import jax.numpy as jnp
from jax import lax
from jax.experimental import pallas as pl
from jax.experimental.pallas import tpu as pltpu
from jax.sharding import Mesh, PartitionSpec as P


BLK = 128
SLAB_BLK = 3
NX, NY, NZ, NC = 4, 4, 8, 2
ROW = ("x", "y")
BF = jnp.bfloat16
F32 = jnp.float32
SMALL = 8 * 1024 * 1024
ORDER = (1, 2, 3, 6, 5, 7, 4)


def slab_kernel(piece, pattern_ref, tile_ref, first_ref, second_ref, held, sems):
    @pl.when(lax.axis_index("z") == 0)
    def _():
        rows, cols = held.shape
        parts = rows // BLK
        copies = []
        for p in range(parts):
            span = pl.ds(p * BLK, BLK)
            copies.append(pltpu.make_async_copy(tile_ref.at[span], held.at[span], sems.at[p]))
            copies[-1].start()
        for p in range(parts):
            copies[p].wait()
            stored = [pattern_ref[p, j] > 0 for j in range(cols // BLK)]
            for row in range(p * BLK, (p + 1) * BLK, 8):
                whose, at = divmod(row, piece)
                z, core = divmod(whose, NC)
                out_ref = (first_ref, second_ref)[core]
                for j in range(cols // BLK):
                    lanes = slice(j * BLK, (j + 1) * BLK)
                    block = held[row : row + 8, lanes]
                    out_ref[z, at : at + 8, lanes] = jnp.where(stored[j], block, jnp.zeros_like(block))


def slab_halves(tile, pattern, slab, piece):
    cols = tile.shape[1]
    return pl.pallas_call(
        lambda *refs: slab_kernel(piece, *refs),
        in_specs=[
            pl.BlockSpec(memory_space=pltpu.SMEM),
            pl.BlockSpec(memory_space=pltpu.HBM),
        ],
        out_specs=[pl.BlockSpec(memory_space=pltpu.VMEM)] * NC,
        out_shape=[pltpu.VMEM((NZ, piece, cols), BF)] * NC,
        scratch_shapes=[pltpu.VMEM((slab, cols), BF), pltpu.SemaphoreType.DMA((SLAB_BLK,))],
        compiler_params=pltpu.CompilerParams(vmem_limit_bytes=SMALL),
        name="slab",
    )(pltpu.with_memory_space_constraint(pattern, pltpu.HBM), pltpu.with_memory_space_constraint(tile, pltpu.HBM))


def grid_place():
    row = lax.axis_index("x") * NY + lax.axis_index("y")
    return row, lax.axis_index("z") * NC + lax.axis_index("core")


def load_kernel(over_mask, dense_mask, over_ref, dense_ref, over_out, dense_out, sems):
    row, col = grid_place()
    diagonal = row == col
    depth, width = over_out.shape
    strips = sems.shape[1]
    tall = depth // strips
    sets = ((over_mask, over_ref, over_out), (dense_mask, dense_ref, dense_out))
    copies = []
    for which, (_, source, held) in enumerate(sets):
        for q in range(strips):
            span = pl.ds(q * tall, tall)
            copies.append(pltpu.make_async_copy(source.at[span], held.at[span], sems.at[which, q]))
            copies[-1].start()
    eye = (
        lax.broadcasted_iota(jnp.int32, (BLK, BLK), 0)
        == lax.broadcasted_iota(jnp.int32, (BLK, BLK), 1)
    ).astype(F32)
    for which, (mask, _, held) in enumerate(sets):
        for q in range(strips):
            copies[which * strips + q].wait()
            for i in range(q * tall // BLK, (q + 1) * tall // BLK):
                for j in range(width // BLK):
                    here = (slice(i * BLK, (i + 1) * BLK), slice(j * BLK, (j + 1) * BLK))
                    block = held[here]
                    held[here] = jnp.where(mask[i, j] > 0, block, jnp.zeros_like(block))

    @pl.when(diagonal)
    def _():
        for i in range(depth // BLK):
            here = (slice(i * BLK, (i + 1) * BLK), slice(i * BLK, (i + 1) * BLK))
            over_out[here] = (over_out[here].astype(F32) + eye).astype(BF)


def in_vmem(x):
    return pltpu.with_memory_space_constraint(x, pltpu.VMEM)


def in_hbm(x):
    return pltpu.with_memory_space_constraint(x, pltpu.HBM)


VMEM_SPEC = pl.BlockSpec(memory_space=pltpu.VMEM)
SMEM_SPEC = pl.BlockSpec(memory_space=pltpu.SMEM)
HBM_SPEC = pl.BlockSpec(memory_space=pltpu.HBM)


def load(margin, density, margin_mask, density_mask):
    return pl.pallas_call(
        load_kernel,
        in_specs=[SMEM_SPEC, SMEM_SPEC, HBM_SPEC, HBM_SPEC],
        out_specs=[VMEM_SPEC, VMEM_SPEC],
        out_shape=[pltpu.VMEM(margin.shape, BF), pltpu.VMEM(density.shape, BF)],
        scratch_shapes=[pltpu.SemaphoreType.DMA((2, 4))],
        compiler_params=pltpu.CompilerParams(vmem_limit_bytes=SMALL),
        cost_estimate=pl.CostEstimate(
            flops=2 * margin.size, bytes_accessed=4 * margin.size, transcendentals=0
        ),
        name="load",
    )(in_hbm(margin_mask), in_hbm(density_mask), in_hbm(margin), in_hbm(density))


def dot_kernel(left_ref, right_ref, out_ref):
    wide = 4 * BLK
    for p in range(right_ref.shape[1] // wide):
        cols = slice(p * wide, (p + 1) * wide)
        out_ref[:, cols] = jnp.dot(
            left_ref[...], right_ref[:, cols], preferred_element_type=F32
        ).astype(out_ref.dtype)


def dot(left, right, dtype):
    rows, depth = left.shape
    cols = right.shape[1]
    return pl.pallas_call(
        dot_kernel,
        in_specs=[VMEM_SPEC, VMEM_SPEC],
        out_specs=VMEM_SPEC,
        out_shape=pltpu.VMEM((rows, cols), dtype),
        compiler_params=pltpu.CompilerParams(vmem_limit_bytes=SMALL),
        cost_estimate=pl.CostEstimate(
            flops=2 * rows * cols * depth, bytes_accessed=2 * rows * (cols + depth), transcendentals=0
        ),
        name="dot",
    )(in_vmem(left), right)


def sum_kernel(parts_ref, out_ref):
    n, _, cols = parts_ref.shape
    for j in range(cols // BLK):
        lanes = slice(j * BLK, (j + 1) * BLK)
        total = parts_ref[0, :, lanes].astype(F32)
        for k in range(1, n):
            total = total + parts_ref[k, :, lanes].astype(F32)
        for k in range(n):
            out_ref[k, :, lanes] = total.astype(BF)


def summed(parts):
    return pl.pallas_call(
        sum_kernel,
        in_specs=[VMEM_SPEC],
        out_specs=VMEM_SPEC,
        out_shape=pltpu.VMEM(parts.shape, BF),
        compiler_params=pltpu.CompilerParams(vmem_limit_bytes=SMALL),
        name="sum",
    )(in_vmem(parts))


def finish_kernel(keep_ref, parts_ref, two_ref, out_ref):
    n, rows, cols = parts_ref.shape
    row, col = grid_place()
    for at in range(0, rows, 8):
        block_row = (col * rows + at) // BLK
        for j in range(cols // BLK):
            lanes = slice(j * BLK, (j + 1) * BLK)
            four = parts_ref[0, at : at + 8, lanes].astype(F32)
            for k in range(1, n):
                four = four + parts_ref[k, at : at + 8, lanes].astype(F32)
            value = 3.0 * two_ref[0, at : at + 8, lanes].astype(F32) - 2.0 * four
            kept = keep_ref[block_row, row * (cols // BLK) + j] > 0
            out_ref[at : at + 8, lanes] = jnp.where(kept, value, jnp.zeros_like(value)).astype(BF)


def finish(parts, two, keep):
    return pl.pallas_call(
        finish_kernel,
        in_specs=[SMEM_SPEC, VMEM_SPEC, VMEM_SPEC],
        out_specs=VMEM_SPEC,
        out_shape=jax.ShapeDtypeStruct(two.shape[1:], BF),
        compiler_params=pltpu.CompilerParams(vmem_limit_bytes=SMALL),
        name="finish",
    )(in_hbm(keep), in_vmem(parts), in_vmem(two))


def exchange(parts, axis):
    return lax.all_to_all(parts, axis, 0, 0, tiled=False)


def swap(x):
    return lax.ppermute(x, "core", [(0, 1), (1, 0)])


def body(density, margin, density_mask, margin_mask, keep_mask):
    side = density.shape[0]
    nr = NX * NY
    z = lax.axis_index("z")
    core = lax.axis_index("core")
    slab = SLAB_BLK * BLK
    piece = slab // (NZ * NC)
    half = NZ * piece

    top = slab_halves(density, density_mask, slab, piece)
    mine = jnp.where(core == 0, top[0], lax.ppermute(top[1], ("z", "core"), [(0, 1)]))
    got = jnp.where(z == 0, mine[0], jnp.zeros_like(mine[0]))
    for d in ORDER:
        dealt = lax.ppermute(mine[d], "z", [(0, d)])
        got = got + dealt
    over, dense = load(margin, density, margin_mask, density_mask)
    own = exchange(jnp.broadcast_to(got[None], (NZ, piece, side)), "z").reshape(half, side)

    def over_rows(first, second):
        part = jnp.concatenate([first, second]).reshape(nr, slab // nr, side)
        return exchange(summed(exchange(part, ROW)), ROW).reshape(slab, side)

    def over_cols(kept, sent):
        part = (kept + sent.astype(F32)).astype(BF)
        return exchange(part.reshape(NZ, piece, side), "z")

    other = swap(own)
    first = dot(own, over, BF)
    left = over_rows(first, dot(other, over, BF))
    sent = swap(dot(left[half:], dense, BF))
    twos = summed(over_cols(dot(left[:half], dense, F32), sent))
    own = exchange(twos, "z").reshape(half, side)
    other = swap(own)
    first = dot(own, over, BF)
    left = over_rows(first, dot(other, over, BF))
    sent = swap(dot(left[half:], dense, BF))
    parts = over_cols(dot(left[:half], dense, F32), sent)
    return finish(parts, twos, keep_mask)


def solution(mesh):
    grid = Mesh(mesh.devices.reshape(NX, NY, NZ, NC), ("x", "y", "z", "core"))
    dn, mg = P(("z", "core"), ROW), P(ROW, ("z", "core"))
    return jax.shard_map(
        body, mesh=grid, in_specs=(dn, mg, dn, mg, P()), out_specs=dn, check_vma=False
    )
```
